32 devices in a mesh: tm: 4 (over x, core), space: 8 (over z, y).
Axes of the slice: x: 2, y: 2, z: 4, core: 2. Of those that a mesh axis runs over, the one named last changes fastest.
Arguments:
- states: float32 [8, 3, 32, 128, 128], P('tm', None, 'space'), may hold values from -6 to 6
- sources: float32 [8, 3, 32, 128, 128], P('tm', None, 'space'), may hold values from -6 to 6
- conductivity: float32 [32, 128, 128], P('space'), may hold values from 0.5 to 4
- gap_tile: int32 [8, 1024, 1], P('tm', 'space'), may hold values from 0 to 7; in each aligned block of 128 rows (0 to 127, 128 to 255, ..., all dimensions but the last counted through in order) at most 32 rows name the same one
- gap_row: int32 [8, 1024], P('tm', 'space'), may hold values from 0 to 127
Outputs:
- new_states: float32 [8, 3, 32, 128, 128], P('tm', None, 'space')
The draws below stay inside these ranges and needn't reach their ends.
Inputs may be any that keep to these rules, and one draw needn't show every extreme that they name: `gap_tile`: in each slice no tile maps more than 32 of its own 128 interface rows to any one tile.
All inputs are finite; a program needn't handle non-finite values.
Results may differ from the reference program's by a relative error of at most 0.0001.
Values sent between devices are 32-bit elements; how exact they have to be, the bound alone decides.
No kernel may reach another device: no remote copies, remote signals or barrier semaphores. Data moves between devices by JAX's collectives and lax.ppermute only.
A program may use at most 128 MiB of HBM per device.

```python
import math
import jax
import jax.numpy as jnp
import numpy as np

CX = 4
CY = 128
CZ = 128
STEPS = 4
SWEEPS = 3
COARSE_SWEEPS = 3
SLICES = 8
NX = 32
CAP = 32
N_SPACE = 8


def place_ends(values, key, low, top_value):
    place = [jax.random.randint(jax.random.fold_in(key, axis), (), 0, length) for axis, length in enumerate(values.shape)]
    widest = values.shape.index(max(values.shape))
    beside = place[:widest] + [(place[widest] + 1) % values.shape[widest]] + place[widest + 1:]
    return values.at[tuple(place)].set(low).at[tuple(beside)].set(top_value)


def level_of(key, dims, split, least, high):
    def one(position, blocks):
        draws = jax.random.uniform(jax.random.fold_in(jax.random.fold_in(key, 6), position), (blocks,), jnp.float32, least / len(split), high / len(split))
        return jnp.repeat(jnp.exp(draws), dims[position] // blocks).reshape((-1,) + (1,) * (len(dims) - position - 1))

    gain = one(*split[0])
    for cut in split[1:]:
        gain = gain * one(*cut)
    return gain


def assign_block(rng, own, number, rows, number_of, top, most, skew):
    ranking = jax.random.permutation(rng, number_of)
    packed, usual = shares(number_of, rows * top, most, skew, True), shares(number_of, rows * top, most, skew, False)
    places = jnp.arange(number_of)

    def named(lengths, offset_by):
        used = int((lengths > 0).sum())
        fixed = max(1, used // 4)
        passed = fixed + (places - fixed + offset_by * (used - fixed)) % max(1, number_of - fixed)
        return jnp.zeros((number_of,), jnp.int32).at[ranking[jnp.where(places < fixed, places, passed)]].set(jnp.asarray(lengths, jnp.int32))

    lengths = jnp.where(number % 4 == 0, named(packed, number // 4), named(usual, number - number // 4 - 1))
    mixed = jax.random.permutation(jax.random.fold_in(own, 3), number_of)
    source_of, taker = mixed[0:number_of // 2 * 2:2], mixed[1:number_of // 2 * 2:2]
    room = jnp.minimum(lengths[source_of] - 1, most - lengths[taker]) // 2
    room = jnp.where((source_of == ranking[0]) | (taker == ranking[0]) | (lengths[taker] == 0), 0, jnp.maximum(room, 0))
    passed = jax.random.randint(jax.random.fold_in(own, 4), (number_of // 2,), 0, 1 << 20) % (room + 1)
    lengths = lengths.at[source_of].add(-passed).at[taker].add(passed)
    items = jnp.searchsorted(jnp.cumsum(lengths), jnp.arange(rows * top), side="right").astype(jnp.int32)
    grid = items.reshape(top, rows).T
    grid = grid[jax.random.permutation(jax.random.fold_in(own, 1), rows)]
    offset_by = jax.random.randint(jax.random.fold_in(own, 2), (rows, 1), 0, top)
    return jnp.take_along_axis(grid, (jnp.arange(top)[None, :] + offset_by) % top, axis=1)


def shares(count, total, limit, slope, full):
    portions = [(1 << 20) // math.isqrt(grade ** slope) + 1 for grade in range(1, count + 1)]
    largest = limit if full else min(limit, max(-(-total // count), total * portions[0] // sum(portions)))
    least = 1 if total - largest >= count - 1 else 0
    given, spare = [largest] + [least] * (count - 1), total - largest - least * (count - 1)
    while spare > 0:
        free = [i for i in range(1, count) if given[i] < largest] or [i for i in range(1, count) if given[i] < limit]
        whole, remaining = sum([portions[i] for i in free]), spare
        for i in free:
            more = min(limit - given[i], max(1, remaining * portions[i] // whole), spare)
            given[i] = given[i] + more
            spare = spare - more
    return np.array(given)


def noise(own_key, extent, scale, bound, pieces=(), dtype=jnp.bfloat16):
    array = scale * jax.random.normal(own_key, extent, jnp.float32)
    if pieces:
        array = array * level_of(own_key, extent, pieces, -0.22, 0.18)
    return jnp.clip(array, -bound, bound).astype(dtype)


def setup_inputs(seed: int = 0) -> dict:
    arg_keys = jax.random.split(jax.random.key(seed), 6)
    states = noise(arg_keys[0], (SLICES, 3, NX, CY, CZ), 1.0, 6.0, ((0, 4), (2, 8)), jnp.float32)
    sources = noise(arg_keys[1], (SLICES, 3, NX, CY, CZ), 1.0, 6.0, ((0, 4), (2, 8)), jnp.float32)
    conductivity = jnp.clip(jnp.exp(math.log(4.0) - 2.0794415 * jax.random.uniform(arg_keys[2], (NX, CY, CZ), jnp.float32) ** level_of(arg_keys[2], (NX, CY, CZ), ((0, 8),), -0.2, 0.2)), 0.5, 4.0)
    gap_tile_keys = jax.random.split(jax.random.fold_in(arg_keys[3], 1), SLICES * (N_SPACE * CY) // CY)
    gap_tile_turns = jax.random.permutation(jax.random.fold_in(arg_keys[3], 3), SLICES * (N_SPACE * CY) // CY)
    gap_tile = jax.vmap(lambda own, number: assign_block(jax.random.fold_in(arg_keys[3], 2), own, number, CY, N_SPACE, 1, CAP, 2))(gap_tile_keys, gap_tile_turns).reshape((SLICES, N_SPACE * CY, 1))
    gap_row = place_ends(jax.random.randint(arg_keys[4], (SLICES, N_SPACE * CY), 0, CY), jax.random.fold_in(arg_keys[4], 1), 0, CY - 1).astype(jnp.int32)
    return dict(states=states, sources=sources, conductivity=conductivity, gap_tile=gap_tile, gap_row=gap_row)


inverse_step = 2.0
gap_gain = 1.0


def neighbours(field):
    padded = jnp.pad(field, ((0, 0), (1, 1), (1, 1), (1, 1)))
    total = padded[:, 2:, 1:-1, 1:-1] + padded[:, :-2, 1:-1, 1:-1]
    total = total + padded[:, 1:-1, 2:, 1:-1] + padded[:, 1:-1, :-2, 1:-1]
    total = total + padded[:, 1:-1, 1:-1, 2:] + padded[:, 1:-1, 1:-1, :-2]
    return total


def jacobi(field, rhs, diag, sweeps):
    for sweep in range(sweeps):
        field = (rhs + neighbours(field)) / diag
    return field


def fine(field, source, conduct, tiles, rows_dst):
    rate = inverse_step * conduct
    dest = (tiles * CY + rows_dst).astype(jnp.int32)
    for step in range(STEPS):
        rows = field[0, ::CX].reshape(N_SPACE * CY, CZ)
        coupled = jax.ops.segment_sum(rows, dest, num_segments=N_SPACE * CY).reshape(N_SPACE, CY, CZ)
        rhs = rate * field + source
        rhs = rhs.at[0, ::CX].add(gap_gain * coupled)
        field = jacobi(field, rhs, rate + 6.0, SWEEPS)
    return field


def coarse(field, source, conduct):
    rate = inverse_step * conduct / STEPS
    return jacobi(field, rate * field + source, rate + 6.0, COARSE_SWEEPS)


def reference(states, sources, conductivity, gap_tile, gap_row):
    ends = []
    jumps = []
    for slot in range(SLICES):
        end = fine(states[slot], sources[slot], conductivity, gap_tile[slot, :, 0], gap_row[slot])
        ends.append(end)
        jumps.append(end - coarse(states[slot], sources[slot], conductivity))
    result = [ends[SLICES - 1]]
    for slot in range(SLICES - 1):
        result.append(coarse(result[slot], sources[slot], conductivity) + jumps[slot])
    return jnp.stack(result)
```

```python
import functools

import jax
import jax.numpy as jnp
from jax import lax
from jax.experimental import pallas as pl
from jax.experimental.pallas import tpu as pltpu
from jax.sharding import PartitionSpec as P

STEPS = 4
SWEEPS = 3

inverse_step = 2.0
gap_gain = 1.0

AXES = ("tm", "space")
HIGHEST = lax.Precision.HIGHEST
PAD = 8


class Layout:
    def __init__(self, times, tiles):
        self.times, self.tiles = times, tiles
        self.all = [(t // 2, t % 2, s // 2, s % 2) for t in range(times) for s in range(tiles)]

    def number(self, ht, c, hs, y):
        return (2 * ht + c) * self.tiles + 2 * hs + y

    def at(self, block, tile):
        return self.number(block // 2, tile % 2, tile // 2, block % 2)

    def relabel(self):
        return [(self.number(h, c, z, y), self.number(h, y, z, c)) for h, c, z, y in self.all]

    def pairs(self, shift_of, blocks=None):
        found = []
        for block in range(self.times) if blocks is None else blocks:
            for tile in range(self.tiles):
                other = shift_of(tile)
                if 0 <= other < self.tiles:
                    found.append((self.at(block, tile), self.at(block, other)))
        return found

    def chip(self, blocks=None):
        return self.pairs(lambda tile: tile ^ 1, blocks)

    def hop(self, blocks=None):
        return self.pairs(lambda tile: tile + 1 if tile % 2 else tile - 1, blocks)

    def down(self):
        return self.pairs(lambda tile: tile - 1)

    def columns(self):
        return [[self.at(block, tile) for tile in range(self.tiles)] for block in range(self.times)]

    def spread(self, k, roles):
        return [
            (self.at(block, tile), self.at(block ^ k, tile))
            for block in range(self.times)
            if block ^ k < roles
            for tile in range(self.tiles)
        ]

    def home(self, k, roles):
        return [
            (self.at(role, tile), (role ^ k) * self.tiles + tile)
            for role in range(roles)
            for tile in range(self.tiles)
        ]


def send(value, pairs):
    return lax.ppermute(value, AXES, pairs)


def f32(*shape):
    return jax.ShapeDtypeStruct(shape, jnp.float32)


def whole(*shape):
    return pl.BlockSpec(shape, lambda i: (0,) * len(shape))


def each(*shape):
    return pl.BlockSpec((None,) + shape, lambda i: (i,) + (0,) * len(shape))


SCALARS = pl.BlockSpec(memory_space=pltpu.SMEM)


def run(kernel, name, grid, in_specs, out_specs, out_shape, scratch=()):
    return pl.pallas_call(
        kernel,
        grid=(grid,),
        in_specs=in_specs,
        out_specs=out_specs,
        out_shape=out_shape,
        scratch_shapes=list(scratch),
        name=name,
    )


def join(flags, own, chip, hop, put):
    wide, count = chip.shape[0], own.shape[0]
    put(wide, own)

    @pl.when(flags[0] == 0)
    def _():
        put(0, hop)
        put(wide + count, chip)

    @pl.when(flags[0] != 0)
    def _():
        put(0, chip)
        put(wide + count, hop)


def extend_kernel(flags, own, chip, hop, out):
    def put(start, ref):
        out[start : start + ref.shape[0]] = ref[...]

    join(flags, own, chip, hop, put)


def conduct_kernel(flags, own, chip, hop, ext, inv_fine, inv_coarse):
    extend_kernel(flags, own, chip, hop, ext)
    wide, count = chip.shape[0], own.shape[0]
    for plane in range(2 * wide + count):
        inside = 1
        if plane < wide:
            inside = flags[1]
        elif plane >= wide + count:
            inside = flags[2]
        mask = jnp.full(ext.shape[1:], inside, jnp.int32) != 0
        rate = inverse_step * ext[plane]
        inv_fine[plane] = jnp.where(mask, 1.0 / (rate + 6.0), 0.0)
        inv_coarse[plane] = jnp.where(mask, 1.0 / (rate / STEPS + 6.0), 0.0)


def sweep(src, dst, base, inv, low, high, shift=0):
    rows, lanes = base.shape[1:]
    lane = lax.broadcasted_iota(jnp.int32, (rows, lanes), 1)
    left_edge, right_edge = lane == 0, lane == lanes - 1

    def plane(p, carry):
        mid = src[p, PAD : PAD + rows, :]
        total = src[p - 1, PAD : PAD + rows, :] + src[p + 1, PAD : PAD + rows, :]
        total = total + (src[p, PAD - 1 : PAD - 1 + rows, :] + src[p, PAD + 1 : PAD + 1 + rows, :])
        left = jnp.where(left_edge, 0.0, pltpu.roll(mid, 1, 1))
        right = jnp.where(right_edge, 0.0, pltpu.roll(mid, lanes - 1, 1))
        new = base[p - 1] + (total + (left + right)) * inv[p - 1]
        if shift:
            dst[p - shift] = new
        else:
            dst[p, PAD : PAD + rows, :] = new
        return carry

    lax.fori_loop(low, high, plane, 0)


def three(start, work, other, base, inv, out):
    planes = start.shape[0]
    sweep(start, work, base, inv, 1, planes - 1)
    sweep(work, other, base, inv, 2, planes - 2)
    sweep(other, out, base, inv, 3, planes - 3, 3)


def clear_edges(*buffers):
    for buffer in buffers:
        rows = buffer.shape[1] - 2 * PAD
        zero = jnp.zeros((buffer.shape[0], PAD, buffer.shape[2]), jnp.float32)
        buffer[:, 0:PAD, :] = zero
        buffer[:, PAD + rows :, :] = zero


def load_field(flags, own, chip, hop, buffer):
    rows = own.shape[1]

    def put(start, ref):
        buffer[start : start + ref.shape[0], PAD : PAD + rows, :] = ref[...]

    join(flags, own, chip, hop, put)


def emit_halos(flags, out, to_chip, to_hop):
    core = flags[0]
    to_chip[...] = out[pl.ds(1 - core, SWEEPS)]
    to_hop[...] = out[pl.ds(core, SWEEPS)]


def fine_kernel(first, last, coupled, *refs):
    refs = list(refs)
    flags, own, chip, hop, source, ext, inv = refs[:7]
    refs = refs[7:]
    if coupled:
        gap, gap_next, refs = refs[0], refs[1], refs[2:]
    if coupled and not last:
        select, refs = refs[0], refs[1:]
    if first:
        inv_coarse, refs = refs[0], refs[1:]
    if last:
        old, refs = refs[0], refs[1:]
    out, refs = refs[0], refs[1:]
    if not last:
        to_chip, to_hop, refs = refs[0], refs[1], refs[2:]
    if coupled and not last:
        packed, refs = refs[0], refs[1:]
    if first:
        old_out, refs = refs[0], refs[1:]
    one, two, three_, base = refs[:4]
    rows = own.shape[1]
    planes = ext.shape[0]
    wide = (planes - own.shape[0]) // 2

    @pl.when(pl.program_id(0) == 0)
    def _():
        clear_edges(one, two, three_)

    load_field(flags, own, chip, hop, one)

    if first:

        def start_coarse(p, carry):
            v = one[p + 1, PAD : PAD + rows, :]
            base[p] = (inverse_step / STEPS) * ext[p] * v * inv_coarse[p]
            return carry

        lax.fori_loop(0, planes, start_coarse, 0)
        three(one, two, three_, base, inv_coarse, old_out)

    def start(p, carry):
        v = one[p + 1, PAD : PAD + rows, :]
        base[p] = (inverse_step * ext[p] * v + source[p]) * inv[p]
        return carry

    lax.fori_loop(0, planes, start, 0)
    if coupled:
        base[wide] = base[wide] + gap_gain * gap[...] * inv[wide]
        above = wide + own.shape[0]
        base[above] = base[above] + gap_gain * gap_next[...] * inv[above]
    three(one, two, three_, base, inv, out)
    if not last:
        emit_halos(flags, out, to_chip, to_hop)
    if coupled and not last:
        pack_into(select, out, packed)
    if last:
        keep = jnp.where(pl.program_id(0) % flags[5] == flags[4], 0.0, 1.0)
        out[...] = out[...] - keep * old[...]


def pack_into(select, field, packed):
    rows = jnp.dot(select[...], field[0], precision=HIGHEST, preferred_element_type=jnp.float32)
    packed[...] = rows.reshape(packed.shape)


def pack_kernel(select, field, packed):
    pack_into(select, field, packed)


def index_kernel(tiles_count, capacity, tile, row, select, dest):
    rows = tile.shape[-1]
    slots = tiles_count * capacity
    lower = lax.broadcasted_iota(jnp.int32, (rows, rows), 0)
    upper = lax.broadcasted_iota(jnp.int32, (rows, rows), 1)
    earlier = (lower < upper).astype(jnp.float32)
    hot = lax.broadcasted_iota(jnp.int32, (tiles_count, rows), 0) == tile[...]
    hot = hot.astype(jnp.float32)
    before = jnp.dot(hot, earlier, precision=HIGHEST, preferred_element_type=jnp.float32)
    position = jnp.sum(before * hot, axis=0, keepdims=True).astype(jnp.int32)
    slot = tile[...] * capacity + position
    chosen = (lax.broadcasted_iota(jnp.int32, (slots, rows), 0) == slot).astype(jnp.float32)
    select[...] = chosen
    wanted = jnp.broadcast_to((row[...] + 1).astype(jnp.float32), (8, rows))
    found = lax.dot_general(
        wanted,
        chosen,
        (((1,), (1,)), ((), ())),
        precision=HIGHEST,
        preferred_element_type=jnp.float32,
    )
    dest[...] = found[0:1]


def unpack_kernel(got, arrived, gap):
    rows, slots = gap.shape[0], got.shape[1]
    want = (lax.broadcasted_iota(jnp.int32, (rows, slots), 0) + 1).astype(jnp.float32)
    receive = (want == got[...]).astype(jnp.float32)
    values = arrived[...].reshape(slots, gap.shape[1])
    gap[...] = jnp.dot(receive, values, precision=HIGHEST, preferred_element_type=jnp.float32)


def fetch(flags, block, slot, parts, buffer, sem):
    for k, part in enumerate(parts):

        @pl.when(flags[3] ^ k == block)
        def _():
            copy = pltpu.make_async_copy(part.at[slot], buffer, sem)
            copy.start()
            copy.wait()


def begin_kernel(block, slot, parts_count, *refs):
    flags, parts = refs[0], refs[1 : 1 + parts_count]
    out, to_chip, to_hop, sem = refs[1 + parts_count :]
    fetch(flags, block, slot, parts, out, sem)
    emit_halos(flags, out, to_chip, to_hop)


def chain_kernel(block, slot, last, parts_count, *refs):
    flags, own, chip, hop, ext, inv = refs[:6]
    parts, refs = refs[6 : 6 + parts_count], list(refs[6 + parts_count :])
    out, refs = refs[0], refs[1:]
    if not last:
        to_chip, to_hop, refs = refs[0], refs[1], refs[2:]
    one, two, three_, base, jump, sem = refs
    rows = own.shape[1]
    planes = ext.shape[0]
    clear_edges(one, two, three_)
    load_field(flags, own, chip, hop, one)

    def start(p, carry):
        v = one[p + 1, PAD : PAD + rows, :]
        base[p] = (inverse_step / STEPS) * ext[p] * v * inv[p]
        return carry

    lax.fori_loop(0, planes, start, 0)
    fetch(flags, block, slot, parts, jump, sem)
    three(one, two, three_, base, inv, out)
    out[...] = out[...] + jump[...]
    if not last:
        emit_halos(flags, out, to_chip, to_hop)


def shards(states, sources, conductivity, gap_tile, gap_row):
    times, tiles = lax.axis_size("tm"), lax.axis_size("space")
    slices, comps, planes, rows, lanes = states.shape
    lay = Layout(times, tiles)
    capacity = max(2, 2 * rows // tiles)
    time_index, tile_index = lax.axis_index("tm"), lax.axis_index("space")
    core = time_index % 2
    block = 2 * (time_index // 2) + tile_index % 2
    tile = 2 * (tile_index // 2) + core
    last_slot = jnp.where(block == times - 1, slices - 1, -1)
    flags = jnp.stack(
        [
            core,
            (tile > 0).astype(jnp.int32),
            (tile < tiles - 1).astype(jnp.int32),
            block,
            last_slot,
            jnp.full((), slices, jnp.int32),
        ]
    ).astype(jnp.int32)
    relabel = lay.relabel()
    edge = SWEEPS - 1
    ext_planes = planes + 2 * edge
    buf_planes = planes + 2 * SWEEPS
    plane = (rows, lanes)

    def cut(value, start, width, axis):
        return lax.dynamic_slice_in_dim(value, start, width, axis)

    def exchange(value, width, axis):
        top = planes - width
        return (
            send(cut(value, top * (1 - core), width, axis), lay.chip()),
            send(cut(value, top * core, width, axis), lay.hop()),
        )

    tables = send(jnp.stack([gap_tile[:, :, 0], gap_row]), relabel)
    state_0 = send(states[:, 0], relabel)
    source_0 = send(sources[:, 0], relabel)
    conduct = send(conductivity, relabel)
    state_1 = send(jnp.moveaxis(states[:, 1:], 1, 0).reshape(-1, planes, *plane), relabel)
    source_1 = send(jnp.moveaxis(sources[:, 1:], 1, 0).reshape(-1, planes, *plane), relabel)

    select, dest = run(
        functools.partial(index_kernel, tiles, capacity),
        "gap_index",
        slices,
        [each(1, rows), each(1, rows)],
        [each(tiles * capacity, rows), each(1, tiles * capacity)],
        [f32(slices, tiles * capacity, rows), f32(slices, 1, tiles * capacity)],
    )(tables[0][:, None], tables[1][:, None])
    groups = lay.columns()

    def trade(value):
        return lax.all_to_all(value, AXES, 0, 0, axis_index_groups=groups, tiled=True)

    dest = jnp.swapaxes(dest.reshape(slices, tiles, capacity), 0, 1)
    got = jnp.swapaxes(trade(dest), 0, 1).reshape(slices, 1, tiles * capacity)

    cond_chip, cond_hop = exchange(conduct, edge, 0)
    ext, inv_fine, inv_coarse = run(
        conduct_kernel,
        "conduct",
        1,
        [SCALARS, whole(planes, *plane), whole(edge, *plane), whole(edge, *plane)],
        [whole(ext_planes, *plane)] * 3,
        [f32(ext_planes, *plane)] * 3,
    )(flags, conduct, cond_chip, cond_hop)

    def widen(value):
        chip, hop = exchange(value, edge, 1)
        return run(
            extend_kernel,
            "widen",
            value.shape[0],
            [SCALARS, each(planes, *plane), each(edge, *plane), each(edge, *plane)],
            each(ext_planes, *plane),
            f32(value.shape[0], ext_planes, *plane),
        )(flags, value, chip, hop)

    wide_0, wide_1 = widen(source_0), widen(source_1)

    buffers = [pltpu.VMEM((buf_planes, rows + 2 * PAD, lanes), jnp.float32)] * 3 + [
        pltpu.VMEM((ext_planes, *plane), jnp.float32)
    ]
    packed_shape = (tiles, slices, capacity, lanes)
    packed_spec = pl.BlockSpec((tiles, None, capacity, lanes), lambda i: (0, i, 0, 0))

    def fine(step, field, chip, hop, source, gaps=None, old=None):
        first, last = step == 0, step == STEPS - 1
        count = field.shape[0]
        args = [flags, field, chip, hop, source, ext, inv_fine]
        ins = [
            SCALARS,
            each(planes, *plane),
            each(SWEEPS, *plane),
            each(SWEEPS, *plane),
            each(ext_planes, *plane),
            whole(ext_planes, *plane),
            whole(ext_planes, *plane),
        ]
        outs, shapes = [each(planes, *plane)], [f32(count, planes, *plane)]
        if gaps is not None:
            args += list(gaps)
            ins += [each(*plane)] * 2
            if not last:
                args.append(select)
                ins.append(each(tiles * capacity, rows))
        if first:
            args.append(inv_coarse)
            ins.append(whole(ext_planes, *plane))
        if last:
            args.append(old)
            ins.append(each(planes, *plane))
        if not last:
            outs += [each(SWEEPS, *plane)] * 2
            shapes += [f32(count, SWEEPS, *plane)] * 2
            if gaps is not None:
                outs.append(packed_spec)
                shapes.append(f32(*packed_shape))
        if first:
            outs.append(each(planes, *plane))
            shapes.append(f32(count, planes, *plane))
        return run(
            functools.partial(fine_kernel, first, last, gaps is not None),
            f"fine_{step}_{int(gaps is not None)}",
            count,
            ins,
            outs,
            shapes,
            buffers,
        )(*args)

    def coupling(packed):
        arrived = trade(packed)
        gap = run(
            unpack_kernel,
            "unpack",
            slices,
            [each(1, tiles * capacity), packed_spec],
            each(*plane),
            f32(slices, *plane),
        )(got, arrived)
        return gap, send(gap, lay.down())

    packed = run(
        pack_kernel,
        "pack",
        slices,
        [each(tiles * capacity, rows), each(planes, *plane)],
        packed_spec,
        f32(*packed_shape),
    )(select, state_0)
    field_0, (chip_0, hop_0) = state_0, exchange(state_0, SWEEPS, 1)
    field_1, (chip_1, hop_1) = state_1, exchange(state_1, SWEEPS, 1)
    old_0 = old_1 = None
    for step in range(STEPS):
        gaps = coupling(packed)
        result_1 = fine(step, field_1, chip_1, hop_1, wide_1, None, old_1)
        result_0 = fine(step, field_0, chip_0, hop_0, wide_0, gaps, old_0)
        field_0, field_1 = result_0[0], result_1[0]
        if step == 0:
            old_0, old_1 = result_0[4], result_1[3]
        if step < STEPS - 1:
            packed = result_0[3]
            chip_0, hop_0 = send(result_0[1], lay.chip()), send(result_0[2], lay.hop())
            chip_1, hop_1 = send(result_1[1], lay.chip()), send(result_1[2], lay.hop())

    jumps = jnp.concatenate([field_0[None], field_1.reshape(comps - 1, slices, planes, *plane)], 0)

    def component(index):
        return lax.dynamic_index_in_dim(jumps, jnp.minimum(index, comps - 1), 0, keepdims=False)

    parts = [component(block)]
    for k in range(1, times):
        parts.append(send(component(block ^ k), lay.spread(k, comps)))
    anywhere = [pl.BlockSpec(memory_space=pl.ANY)] * times
    halo_specs = [whole(SWEEPS, *plane)] * 2
    halo_shapes = [f32(SWEEPS, *plane)] * 2
    dma = pltpu.SemaphoreType.DMA(())
    roles = range(comps)
    total = times * slices
    new, chip, hop = run(
        functools.partial(begin_kernel, times - 1, slices - 1, times),
        "begin",
        1,
        [SCALARS] + anywhere,
        [whole(planes, *plane)] + halo_specs,
        [f32(planes, *plane)] + halo_shapes,
        [dma],
    )(flags, *parts)
    news = [new]
    for j in range(total - 1):
        chip, hop = send(chip, lay.chip(roles)), send(hop, lay.hop(roles))
        last = j == total - 2
        result = run(
            functools.partial(chain_kernel, j // slices, j % slices, last, times),
            f"chain_{j}",
            1,
            [SCALARS, whole(planes, *plane)] + halo_specs + [whole(ext_planes, *plane)] * 2 + anywhere,
            [whole(planes, *plane)] + ([] if last else halo_specs),
            [f32(planes, *plane)] + ([] if last else halo_shapes),
            buffers + [pltpu.VMEM((planes, *plane), jnp.float32), dma],
        )(flags, new, chip, hop, ext, inv_coarse, *parts)
        new = result[0]
        if not last:
            chip, hop = result[1:]
        news.append(new)

    ready = jnp.stack(news).reshape(times, slices, planes, *plane)
    back = jnp.stack(
        [
            send(lax.dynamic_index_in_dim(ready, block ^ k, 0, keepdims=False), lay.home(k, comps))
            for k in range(times)
        ]
    )
    return jnp.stack(
        [
            lax.dynamic_index_in_dim(back, time_index ^ comp, 0, keepdims=False)
            for comp in range(comps)
        ],
        axis=1,
    )


def solution(mesh):
    placed = (
        P("tm", None, "space", None, None),
        P("tm", None, "space", None, None),
        P("space", None, None),
        P("tm", "space", None),
        P("tm", "space"),
    )
    return jax.shard_map(
        shards,
        mesh=mesh,
        in_specs=placed,
        out_specs=P("tm", None, "space", None, None),
        check_vma=False,
    )
```

```python
import functools

import jax
import jax.numpy as jnp
from jax import lax
from jax.experimental import pallas as pl
from jax.experimental.pallas import tpu as pltpu
from jax.sharding import PartitionSpec as P

STEPS = 4
SWEEPS = 3

inverse_step = 2.0
gap_gain = 1.0

AXES = ("tm", "space")
HIGHEST = lax.Precision.HIGHEST
PAD = 8


class Layout:
    def __init__(self, times, tiles):
        self.times, self.tiles = times, tiles
        self.all = [(t // 2, t % 2, s // 2, s % 2) for t in range(times) for s in range(tiles)]

    def number(self, ht, c, hs, y):
        return (2 * ht + c) * self.tiles + 2 * hs + y

    def at(self, block, tile):
        return self.number(block // 2, tile % 2, tile // 2, block % 2)

    def relabel(self):
        return [(self.number(h, c, z, y), self.number(h, y, z, c)) for h, c, z, y in self.all]

    def pairs(self, shift_of, blocks=None):
        found = []
        for block in range(self.times) if blocks is None else blocks:
            for tile in range(self.tiles):
                other = shift_of(tile)
                if 0 <= other < self.tiles:
                    found.append((self.at(block, tile), self.at(block, other)))
        return found

    def chip(self, blocks=None):
        return self.pairs(lambda tile: tile ^ 1, blocks)

    def hop(self, blocks=None):
        return self.pairs(lambda tile: tile + 1 if tile % 2 else tile - 1, blocks)

    def down(self):
        return self.pairs(lambda tile: tile - 1)

    def columns(self):
        return [[self.at(block, tile) for tile in range(self.tiles)] for block in range(self.times)]

    def spread(self, k, roles):
        return [
            (self.at(role ^ k, tile), self.at(role, tile))
            for role in roles
            for tile in range(self.tiles)
            if role ^ k < self.times
        ]

    def gather(self, block):
        return [(self.at(block, tile), self.at(0, tile)) for tile in range(self.tiles)]

    def home(self, k, roles):
        return [
            (self.at(role, tile), (role ^ k) * self.tiles + tile)
            for role in range(roles)
            for tile in range(self.tiles)
            if role ^ k < self.times - 1
        ]

    def home_last(self, role):
        return [
            (self.at(role, tile), (self.times - 1) * self.tiles + tile)
            for tile in range(self.tiles)
        ]


def send(value, pairs):
    return lax.ppermute(value, AXES, pairs)


def f32(*shape):
    return jax.ShapeDtypeStruct(shape, jnp.float32)


def whole(*shape):
    return pl.BlockSpec(shape, lambda i: (0,) * len(shape))


def each(*shape):
    return pl.BlockSpec((None,) + shape, lambda i: (i,) + (0,) * len(shape))


SCALARS = pl.BlockSpec(memory_space=pltpu.SMEM)


def run(kernel, name, grid, in_specs, out_specs, out_shape, scratch=()):
    return pl.pallas_call(
        kernel,
        grid=(grid,),
        in_specs=in_specs,
        out_specs=out_specs,
        out_shape=out_shape,
        scratch_shapes=list(scratch),
        name=name,
    )


def join(flags, own, chip, hop, put):
    wide, count = chip.shape[0], own.shape[0]
    put(wide, own)

    @pl.when(flags[0] == 0)
    def _():
        put(0, hop)
        put(wide + count, chip)

    @pl.when(flags[0] != 0)
    def _():
        put(0, chip)
        put(wide + count, hop)


def extend_kernel(flags, own, chip, hop, out):
    def put(start, ref):
        out[start : start + ref.shape[0]] = ref[...]

    join(flags, own, chip, hop, put)


def widen_kernel(flags, own, chip, hop, inv, out):
    def put(start, ref):
        stop = start + ref.shape[0]
        out[start:stop] = ref[...] * inv[start:stop]

    join(flags, own, chip, hop, put)


def conduct_kernel(flags, own, chip, hop, fine_rate, fine_inv, coarse_rate, coarse_inv):
    def put(start, ref):
        fine_rate[start : start + ref.shape[0]] = ref[...]

    join(flags, own, chip, hop, put)
    wide, count = chip.shape[0], own.shape[0]
    for plane in range(2 * wide + count):
        inside = 1
        if plane < wide:
            inside = flags[1]
        elif plane >= wide + count:
            inside = flags[2]
        mask = jnp.full(own.shape[1:], inside, jnp.int32) != 0
        rate = inverse_step * fine_rate[plane]
        inv = jnp.where(mask, 1.0 / (rate + 6.0), 0.0)
        fine_inv[plane] = inv
        fine_rate[plane] = rate * inv
        rate = rate / STEPS
        inv = jnp.where(mask, 1.0 / (rate + 6.0), 0.0)
        coarse_inv[plane] = inv
        coarse_rate[plane] = rate * inv


def sweep(src, base, inv, low, high, emit):
    rows, lanes = inv.shape[1:]
    lane = lax.broadcasted_iota(jnp.int32, (rows, lanes), 1)
    left_edge, right_edge = lane == 0, lane == lanes - 1
    for p in range(low, high):
        mid = src[p, PAD : PAD + rows, :]
        total = src[p - 1, PAD : PAD + rows, :] + src[p + 1, PAD : PAD + rows, :]
        total = total + (src[p, PAD - 1 : PAD - 1 + rows, :] + src[p, PAD + 1 : PAD + 1 + rows, :])
        left = jnp.where(left_edge, 0.0, pltpu.roll(mid, 1, 1))
        right = jnp.where(right_edge, 0.0, pltpu.roll(mid, lanes - 1, 1))
        emit(p, base(p - 1, mid) + (total + (left + right)) * inv[p - 1])


def three(start, work, other, keep, first_base, inv, finish):
    planes, rows = start.shape[0], inv.shape[1]

    def make(p, mid):
        value = first_base(p, mid)
        if 1 <= p < inv.shape[0] - 1:
            keep[p] = value
        return value

    def to(buffer):
        def emit(p, value):
            buffer[p, PAD : PAD + rows, :] = value

        return emit

    sweep(start, make, inv, 1, planes - 1, to(work))
    sweep(work, lambda p, mid: keep[p], inv, 2, planes - 2, to(other))
    sweep(other, lambda p, mid: keep[p], inv, SWEEPS, planes - SWEEPS, lambda p, v: finish(p - SWEEPS, v))


def clear_edges(*buffers):
    for buffer in buffers:
        rows = buffer.shape[1] - 2 * PAD
        zero = jnp.zeros((buffer.shape[0], PAD, buffer.shape[2]), jnp.float32)
        buffer[:, 0:PAD, :] = zero
        buffer[:, PAD + rows :, :] = zero


def load_field(flags, own, chip, hop, buffer):
    rows = own.shape[1]

    def put(start, ref):
        buffer[start : start + ref.shape[0], PAD : PAD + rows, :] = ref[...]

    join(flags, own, chip, hop, put)


def emit_halos(flags, out, to_chip, to_hop):
    core = flags[0]
    to_chip[...] = out[pl.ds(1 - core, SWEEPS)]
    to_hop[...] = out[pl.ds(core, SWEEPS)]


def fine_kernel(first, last, coupled, per, *refs):
    refs = list(refs)
    flags, own, chip, hop, source, rate, inv = refs[:7]
    refs = refs[7:]
    if coupled:
        got, arrived, refs = refs[0], refs[1], refs[2:]
    if coupled and not last:
        select, refs = refs[0], refs[1:]
    if first:
        coarse_rate, coarse_inv, refs = refs[0], refs[1], refs[2:]
    if last:
        old, refs = refs[0], refs[1:]
    out, refs = refs[0], refs[1:]
    if not last:
        to_chip, to_hop, refs = refs[0], refs[1], refs[2:]
    if coupled and not last:
        packed, refs = refs[0], refs[1:]
    if first:
        old_out, refs = refs[0], refs[1:]
    one, two, other, keep = refs[:4]
    wide = (inv.shape[0] - own.shape[0]) // 2

    @pl.when(pl.program_id(0) == 0)
    def _():
        clear_edges(one, two, other)

    load_field(flags, own, chip, hop, one)
    if first:

        def put_old(p, value):
            old_out[p] = value

        three(one, two, other, keep, lambda p, mid: coarse_rate[p] * mid, coarse_inv, put_old)

    gaps = {}
    if coupled:
        for which in range(2):
            gap = unpacked(got, arrived, which, own.shape[1])
            gaps[wide + which * own.shape[0]] = gap_gain * gap

    def base(p, mid):
        value = rate[p] * mid + source[p]
        if p in gaps:
            value = value + gaps[p] * inv[p]
        return value

    factor = jnp.where(pl.program_id(0) // per == flags[4], 0.0, 1.0)

    def put(p, value):
        if last:
            value = value - factor * old[p]
        out[p] = value

    three(one, two, other, keep, base, inv, put)
    if not last:
        emit_halos(flags, out, to_chip, to_hop)
    if coupled and not last:
        pack_into(select, out, packed)


def unpacked(got, arrived, which, rows):
    slots = got.shape[1]
    want = (lax.broadcasted_iota(jnp.int32, (rows, slots), 0) + 1).astype(jnp.float32)
    receive = (want == got[which : which + 1]).astype(jnp.float32)
    values = arrived[:, which].reshape(slots, arrived.shape[-1])
    return jnp.dot(receive, values, precision=HIGHEST, preferred_element_type=jnp.float32)


def pack_into(select, field, packed):
    rows = jnp.dot(select[...], field[0], precision=HIGHEST, preferred_element_type=jnp.float32)
    tiles, _, capacity, lanes = packed.shape
    rows = rows.reshape(tiles, capacity, lanes)
    packed[:, 0] = rows
    packed[: tiles - 1, 1] = rows[1:]
    packed[tiles - 1, 1] = jnp.zeros((capacity, lanes), jnp.float32)


def pack_kernel(select, field, packed):
    pack_into(select, field, packed)


def index_kernel(tiles_count, capacity, tile, row, select, dest):
    rows = tile.shape[-1]
    slots = tiles_count * capacity
    lower = lax.broadcasted_iota(jnp.int32, (rows, rows), 0)
    upper = lax.broadcasted_iota(jnp.int32, (rows, rows), 1)
    earlier = (lower < upper).astype(jnp.float32)
    hot = lax.broadcasted_iota(jnp.int32, (tiles_count, rows), 0) == tile[...]
    hot = hot.astype(jnp.float32)
    before = jnp.dot(hot, earlier, precision=HIGHEST, preferred_element_type=jnp.float32)
    position = jnp.sum(before * hot, axis=0, keepdims=True).astype(jnp.int32)
    slot = tile[...] * capacity + position
    chosen = (lax.broadcasted_iota(jnp.int32, (slots, rows), 0) == slot).astype(jnp.float32)
    select[...] = chosen
    wanted = jnp.broadcast_to((row[...] + 1).astype(jnp.float32), (8, rows))
    found = lax.dot_general(
        wanted,
        chosen,
        (((1,), (1,)), ((), ())),
        precision=HIGHEST,
        preferred_element_type=jnp.float32,
    )
    dest[...] = found[0:1]


def start_fetch(flags, choices, buffer, sem):
    count = len(choices)
    for role, (part, index) in enumerate(choices):
        mine = flags[3] == role if role < count - 1 else flags[3] >= role

        @pl.when(mine)
        def _():
            pltpu.make_async_copy(part.at[index], buffer, sem).start()

    part, index = choices[0]
    return pltpu.make_async_copy(part.at[index], buffer, sem)


def begin_kernel(indices, *refs):
    count = len(indices)
    flags, parts = refs[0], refs[1 : 1 + count]
    out, to_chip, to_hop, sem = refs[1 + count :]
    start_fetch(flags, list(zip(parts, indices)), out, sem).wait()
    emit_halos(flags, out, to_chip, to_hop)


def chain_kernel(indices, last, *refs):
    count = len(indices)
    flags, own, chip, hop, rate, inv = refs[:6]
    parts, refs = refs[6 : 6 + count], list(refs[6 + count :])
    out, refs = refs[0], refs[1:]
    if not last:
        to_chip, to_hop, refs = refs[0], refs[1], refs[2:]
    one, two, other, keep, jump, sem = refs
    copy = start_fetch(flags, list(zip(parts, indices)), jump, sem)
    clear_edges(one, two, other)
    load_field(flags, own, chip, hop, one)

    def put(p, value):
        if p == 0:
            copy.wait()
        out[p] = value + jump[p]

    three(one, two, other, keep, lambda p, mid: rate[p] * mid, inv, put)
    if not last:
        emit_halos(flags, out, to_chip, to_hop)


def shards(states, sources, conductivity, gap_tile, gap_row):
    times, tiles = lax.axis_size("tm"), lax.axis_size("space")
    slices, comps, planes, rows, lanes = states.shape
    lay = Layout(times, tiles)
    capacity = max(2, 2 * rows // tiles)
    time_index, tile_index = lax.axis_index("tm"), lax.axis_index("space")
    core = time_index % 2
    block = 2 * (time_index // 2) + tile_index % 2
    tile = 2 * (tile_index // 2) + core
    last_slot = jnp.where(block == times - 1, slices - 1, -1)
    flags = jnp.stack(
        [
            core,
            (tile > 0).astype(jnp.int32),
            (tile < tiles - 1).astype(jnp.int32),
            block,
            last_slot,
            jnp.full((), slices, jnp.int32),
        ]
    ).astype(jnp.int32)
    relabel = lay.relabel()
    edge = SWEEPS - 1
    ext_planes = planes + 2 * edge
    buf_planes = planes + 2 * SWEEPS
    plane = (rows, lanes)

    def cut(value, start, width, axis):
        return lax.dynamic_slice_in_dim(value, start, width, axis)

    def exchange(value, width, axis):
        top = planes - width
        return (
            send(cut(value, top * (1 - core), width, axis), lay.chip()),
            send(cut(value, top * core, width, axis), lay.hop()),
        )

    tables = send(jnp.stack([gap_tile[:, :, 0], gap_row]), relabel)
    state_0 = send(states[:, 0], relabel)
    conduct = send(conductivity, relabel)
    source_0 = send(sources[:, 0], relabel)
    state_1 = send(states[:, 1:].reshape(-1, planes, *plane), relabel)
    source_1 = send(sources[:, 1:].reshape(-1, planes, *plane), relabel)

    slots = tiles * capacity
    select, dest = run(
        functools.partial(index_kernel, tiles, capacity),
        "gap_index",
        slices,
        [each(1, rows), each(1, rows)],
        [each(slots, rows), each(1, slots)],
        [f32(slices, slots, rows), f32(slices, 1, slots)],
    )(tables[0][:, None], tables[1][:, None])
    groups = lay.columns()

    def trade(value):
        return lax.all_to_all(value, AXES, 0, 0, axis_index_groups=groups, tiled=True)

    dest = jnp.swapaxes(dest.reshape(slices, tiles, capacity), 0, 1)
    above = jnp.concatenate([dest[1:], jnp.zeros_like(dest[:1])], 0)
    got = trade(jnp.stack([dest, above], 2))
    got = got.transpose(1, 2, 0, 3).reshape(slices, 2, slots)

    cond_chip, cond_hop = exchange(conduct, edge, 0)
    fine_rate, fine_inv, coarse_rate, coarse_inv = run(
        conduct_kernel,
        "conduct",
        1,
        [SCALARS, whole(planes, *plane), whole(edge, *plane), whole(edge, *plane)],
        [whole(ext_planes, *plane)] * 4,
        [f32(ext_planes, *plane)] * 4,
    )(flags, conduct, cond_chip, cond_hop)

    def widen(value):
        chip, hop = exchange(value, edge, 1)
        return run(
            widen_kernel,
            "widen",
            value.shape[0],
            [SCALARS, each(planes, *plane)]
            + [each(edge, *plane)] * 2
            + [whole(ext_planes, *plane)],
            each(ext_planes, *plane),
            f32(value.shape[0], ext_planes, *plane),
        )(flags, value, chip, hop, fine_inv)

    buffers = [pltpu.VMEM((buf_planes, rows + 2 * PAD, lanes), jnp.float32)] * 3 + [
        pltpu.VMEM((ext_planes, *plane), jnp.float32)
    ]
    packed_shape = (tiles, slices, 2, capacity, lanes)
    packed_spec = pl.BlockSpec((tiles, None, 2, capacity, lanes), lambda i: (0, i, 0, 0, 0))

    def fine(step, field, chip, hop, source, arrived=None, old=None):
        first, last = step == 0, step == STEPS - 1
        count = field.shape[0]
        coupled = arrived is not None
        args = [flags, field, chip, hop, source, fine_rate, fine_inv]
        ins = [
            SCALARS,
            each(planes, *plane),
            each(SWEEPS, *plane),
            each(SWEEPS, *plane),
            each(ext_planes, *plane),
            whole(ext_planes, *plane),
            whole(ext_planes, *plane),
        ]
        outs, shapes = [each(planes, *plane)], [f32(count, planes, *plane)]
        if coupled:
            args += [got, arrived]
            ins += [each(2, slots), packed_spec]
            if not last:
                args.append(select)
                ins.append(each(slots, rows))
        if first:
            args += [coarse_rate, coarse_inv]
            ins += [whole(ext_planes, *plane)] * 2
        if last:
            args.append(old)
            ins.append(each(planes, *plane))
        if not last:
            outs += [each(SWEEPS, *plane)] * 2
            shapes += [f32(count, SWEEPS, *plane)] * 2
            if coupled:
                outs.append(packed_spec)
                shapes.append(f32(*packed_shape))
        if first:
            outs.append(each(planes, *plane))
            shapes.append(f32(count, planes, *plane))
        return run(
            functools.partial(fine_kernel, first, last, coupled, count // slices),
            f"fine_{step}_{int(coupled)}",
            count,
            ins,
            outs,
            shapes,
            buffers,
        )(*args)

    packed = run(
        pack_kernel,
        "pack",
        slices,
        [each(slots, rows), each(planes, *plane)],
        packed_spec,
        f32(*packed_shape),
    )(select, state_0)
    field_0, (chip_0, hop_0), wide_0 = state_0, exchange(state_0, SWEEPS, 1), widen(source_0)
    field_1, (chip_1, hop_1), wide_1 = state_1, exchange(state_1, SWEEPS, 1), widen(source_1)
    old_0 = old_1 = None
    for step in range(STEPS):
        arrived = trade(packed)
        result_1 = fine(step, field_1, chip_1, hop_1, wide_1, None, old_1)
        result_0 = fine(step, field_0, chip_0, hop_0, wide_0, arrived, old_0)
        field_0, field_1 = result_0[0], result_1[0]
        if step == 0:
            old_0, old_1 = result_0[4], result_1[3]
        if step < STEPS - 1:
            packed = result_0[3]
            chip_0, hop_0 = send(result_0[1], lay.chip()), send(result_0[2], lay.hop())
            chip_1, hop_1 = send(result_1[1], lay.chip()), send(result_1[2], lay.hop())

    others = comps - 1
    by_comp = field_1.reshape(slices, others, planes, *plane)

    def component(role):
        index = jnp.clip(role - 1, 0, others - 1)
        return lax.dynamic_index_in_dim(by_comp, index, 1, keepdims=False)

    spread = {k: send(component(block ^ k), lay.spread(k, range(1, comps))) for k in range(1, times)}
    end = times - 1
    gathered = {}
    for slot in reversed(range(slices)):
        gathered[end, slot] = (send(field_0[slot : slot + 1], lay.gather(end)), 0)
    for source in range(end):
        whole_block = field_0 if source == 0 else send(field_0, lay.gather(source))
        for slot in range(slices):
            gathered[source, slot] = (whole_block, slot)

    def choices(source, slot):
        found = [gathered[source, slot]]
        for role in range(1, comps):
            if role == source:
                found.append((field_1, slot * others + role - 1))
            else:
                found.append((spread[role ^ source], slot))
        return [part for part, _ in found], [index for _, index in found]

    anywhere = [pl.BlockSpec(memory_space=pl.ANY)] * comps
    halo_specs = [whole(SWEEPS, *plane)] * 2
    halo_shapes = [f32(SWEEPS, *plane)] * 2
    dma = pltpu.SemaphoreType.DMA(())
    roles = range(comps)
    total = times * slices
    parts, indices = choices(end, slices - 1)
    new, chip, hop = run(
        functools.partial(begin_kernel, indices),
        "begin",
        1,
        [SCALARS] + anywhere,
        [whole(planes, *plane)] + halo_specs,
        [f32(planes, *plane)] + halo_shapes,
        [dma],
    )(flags, *parts)
    news = [new]
    for j in range(total - 1):
        chip, hop = send(chip, lay.chip(roles)), send(hop, lay.hop(roles))
        last = j == total - 2
        parts, indices = choices(j // slices, j % slices)
        result = run(
            functools.partial(chain_kernel, indices, last),
            f"chain_{j}",
            1,
            [SCALARS, whole(planes, *plane)]
            + halo_specs
            + [whole(ext_planes, *plane)] * 2
            + anywhere,
            [whole(planes, *plane)] + ([] if last else halo_specs),
            [f32(planes, *plane)] + ([] if last else halo_shapes),
            buffers + [pltpu.VMEM((planes, *plane), jnp.float32), dma],
        )(flags, new, chip, hop, coarse_rate, coarse_inv, *parts)
        new = result[0]
        if not last:
            chip, hop = result[1:]
        news.append(new)

    early = total - slices
    ready = jnp.stack(news[:early]).reshape(end, slices, planes, *plane)
    back = []
    for k in range(times):
        value = lax.dynamic_index_in_dim(ready, jnp.minimum(block ^ k, end - 1), 0, keepdims=False)
        back.append(send(value, lay.home(k, comps)))
    back = jnp.stack(back)
    result = []
    for comp in range(comps):
        pairs = lay.home_last(comp)
        late = jnp.stack([send(news[early + slot], pairs) for slot in range(slices)])
        soon = lax.dynamic_index_in_dim(back, time_index ^ comp, 0, keepdims=False)
        result.append(jnp.where(time_index == end, late, soon))
    return jnp.stack(result, axis=1)


def solution(mesh):
    placed = (
        P("tm", None, "space", None, None),
        P("tm", None, "space", None, None),
        P("space", None, None),
        P("tm", "space", None),
        P("tm", "space"),
    )
    return jax.shard_map(
        shards,
        mesh=mesh,
        in_specs=placed,
        out_specs=P("tm", None, "space", None, None),
        check_vma=False,
    )
```

```python
import functools

import jax
import jax.numpy as jnp
from jax import lax
from jax.experimental import pallas as pl
from jax.experimental.pallas import tpu as pltpu
from jax.sharding import PartitionSpec as P


STEPS = 4
SWEEPS = 3

inverse_step = 2.0
gap_gain = 1.0

AXES = ("tm", "space")
HIGHEST = lax.Precision.HIGHEST
PAD = 8


class Layout:
    def __init__(self, times, tiles):
        self.times, self.tiles = times, tiles
        self.all = [(t // 2, t % 2, s // 2, s % 2) for t in range(times) for s in range(tiles)]

    def number(self, ht, c, hs, y):
        return (2 * ht + c) * self.tiles + 2 * hs + y

    def at(self, block, tile):
        return self.number(block // 2, tile % 2, tile // 2, block % 2)

    def relabel(self):
        return [(self.number(h, c, z, y), self.number(h, y, z, c)) for h, c, z, y in self.all]

    def pairs(self, shift_of, blocks=None):
        found = []
        for block in range(self.times) if blocks is None else blocks:
            for tile in range(self.tiles):
                other = shift_of(tile)
                if 0 <= other < self.tiles:
                    found.append((self.at(block, tile), self.at(block, other)))
        return found

    def chip(self, blocks=None):
        return self.pairs(lambda tile: tile ^ 1, blocks)

    def hop(self, blocks=None):
        return self.pairs(lambda tile: tile + 1 if tile % 2 else tile - 1, blocks)

    def down(self):
        return self.pairs(lambda tile: tile - 1)

    def columns(self):
        return [[self.at(block, tile) for tile in range(self.tiles)] for block in range(self.times)]

    def spread(self, k, roles):
        return [
            (self.at(role ^ k, tile), self.at(role, tile))
            for role in roles
            for tile in range(self.tiles)
            if role ^ k < self.times
        ]

    def move(self, block, role):
        return [(self.at(block, tile), self.at(role, tile)) for tile in range(self.tiles)]

    def home(self, k, roles):
        return [
            (self.at(role, tile), (role ^ k) * self.tiles + tile)
            for role in range(roles)
            for tile in range(self.tiles)
            if role ^ k < self.times - 1
        ]

    def home_last(self, role):
        return [
            (self.at(role, tile), (self.times - 1) * self.tiles + tile)
            for tile in range(self.tiles)
        ]


def send(value, pairs):
    return lax.ppermute(value, AXES, pairs)


def f32(*shape):
    return jax.ShapeDtypeStruct(shape, jnp.float32)


def whole(*shape):
    return pl.BlockSpec(shape, lambda i: (0,) * len(shape))


def each(*shape, at=0):
    return pl.BlockSpec((None,) + shape, lambda i: (i + at,) + (0,) * len(shape))


SCALARS = pl.BlockSpec(memory_space=pltpu.SMEM)


def run(kernel, grid, in_specs, out_specs, out_shape, scratch=()):
    return pl.pallas_call(
        kernel,
        grid=(grid,),
        in_specs=in_specs,
        out_specs=out_specs,
        out_shape=out_shape,
        scratch_shapes=list(scratch),
    )


def join(flags, own, chip, hop, wide, put):
    count, held = own.shape[0], chip.shape[0]
    put(wide, own[...])

    @pl.when(flags[0] == 0)
    def _():
        put(0, hop[held - wide :])
        put(wide + count, chip[:wide])

    @pl.when(flags[0] != 0)
    def _():
        put(0, chip[held - wide :])
        put(wide + count, hop[:wide])


def widen_kernel(flags, own, chip, hop, inv, out):
    def put(start, planes):
        stop = start + planes.shape[0]
        out[start:stop] = planes * inv[start:stop]

    join(flags, own, chip, hop, (out.shape[0] - own.shape[0]) // 2, put)


def conduct_kernel(flags, own, chip, hop, fine_rate, fine_inv, coarse_rate, coarse_inv):
    def put(start, planes):
        fine_rate[start : start + planes.shape[0]] = planes

    count = own.shape[0]
    wide = (fine_rate.shape[0] - count) // 2
    join(flags, own, chip, hop, wide, put)
    for plane in range(2 * wide + count):
        inside = 1
        if plane < wide:
            inside = flags[1]
        elif plane >= wide + count:
            inside = flags[2]
        mask = jnp.full(own.shape[1:], inside, jnp.int32) != 0
        rate = inverse_step * fine_rate[plane]
        inv = jnp.where(mask, 1.0 / (rate + 6.0), 0.0)
        fine_inv[plane] = inv
        fine_rate[plane] = rate * inv
        rate = rate / STEPS
        inv = jnp.where(mask, 1.0 / (rate + 6.0), 0.0)
        coarse_inv[plane] = inv
        coarse_rate[plane] = rate * inv


def sweep(src, base, inv, low, high, emit):
    rows, lanes = inv.shape[1:]
    lane = lax.broadcasted_iota(jnp.int32, (rows, lanes), 1)
    left_edge, right_edge = lane == 0, lane == lanes - 1
    for p in range(low, high):
        mid = src[p, PAD : PAD + rows, :]
        total = src[p - 1, PAD : PAD + rows, :] + src[p + 1, PAD : PAD + rows, :]
        total = total + (src[p, PAD - 1 : PAD - 1 + rows, :] + src[p, PAD + 1 : PAD + 1 + rows, :])
        left = jnp.where(left_edge, 0.0, pltpu.roll(mid, 1, 1))
        right = jnp.where(right_edge, 0.0, pltpu.roll(mid, lanes - 1, 1))
        emit(p, base(p - 1, mid) + (total + (left + right)) * inv[p - 1])


def three(start, work, other, keep, first_base, inv, finish):
    planes, rows = start.shape[0], inv.shape[1]

    def make(p, mid):
        value = first_base(p, mid)
        if 1 <= p < inv.shape[0] - 1:
            keep[p] = value
        return value

    def to(buffer):
        def emit(p, value):
            buffer[p, PAD : PAD + rows, :] = value

        return emit

    sweep(start, make, inv, 1, planes - 1, to(work))
    sweep(work, lambda p, mid: keep[p], inv, 2, planes - 2, to(other))
    sweep(other, lambda p, mid: keep[p], inv, SWEEPS, planes - SWEEPS, lambda p, v: finish(p - SWEEPS, v))


def clear_edges(*buffers):
    for buffer in buffers:
        rows = buffer.shape[1] - 2 * PAD
        zero = jnp.zeros((buffer.shape[0], PAD, buffer.shape[2]), jnp.float32)
        buffer[:, 0:PAD, :] = zero
        buffer[:, PAD + rows :, :] = zero


def load_field(flags, own, chip, hop, buffer):
    rows = own.shape[1]

    def put(start, planes):
        buffer[start : start + planes.shape[0], PAD : PAD + rows, :] = planes

    join(flags, own, chip, hop, chip.shape[0], put)


def emit_halos(flags, out, to_chip, to_hop):
    core = flags[0]
    to_chip[...] = out[pl.ds(1 - core, SWEEPS)]
    to_hop[...] = out[pl.ds(core, SWEEPS)]


def fine_kernel(first, last, coupled, per, *refs):
    refs = list(refs)
    flags, own, chip, hop, source, rate, inv = refs[:7]
    refs = refs[7:]
    if coupled:
        got, arrived, refs = refs[0], refs[1], refs[2:]
    if coupled and not last:
        select, refs = refs[0], refs[1:]
    if first:
        coarse_rate, coarse_inv, refs = refs[0], refs[1], refs[2:]
    if last:
        old, refs = refs[0], refs[1:]
    out, refs = refs[0], refs[1:]
    if not last:
        to_chip, to_hop, refs = refs[0], refs[1], refs[2:]
    if coupled and not last:
        packed, refs = refs[0], refs[1:]
    if first:
        old_out, refs = refs[0], refs[1:]
    one, two, other, keep = refs[:4]
    wide = (inv.shape[0] - own.shape[0]) // 2

    @pl.when(pl.program_id(0) == 0)
    def _():
        clear_edges(one, two, other)

    load_field(flags, own, chip, hop, one)
    if first:

        def put_old(p, value):
            old_out[p] = value

        three(one, two, other, keep, lambda p, mid: coarse_rate[p] * mid, coarse_inv, put_old)

    gaps = {}
    if coupled:
        for which in range(2):
            gap = unpacked(got, arrived, which, own.shape[1])
            gaps[wide + which * own.shape[0]] = gap_gain * gap

    def base(p, mid):
        value = rate[p] * mid + source[p]
        if p in gaps:
            value = value + gaps[p] * inv[p]
        return value

    factor = jnp.where(pl.program_id(0) // per == flags[4], 0.0, 1.0)

    def put(p, value):
        if last:
            value = value - factor * old[p]
        out[p] = value

    three(one, two, other, keep, base, inv, put)
    if not last:
        emit_halos(flags, out, to_chip, to_hop)
    if coupled and not last:
        pack_into(select, out, packed)


def unpacked(got, arrived, which, rows):
    slots = got.shape[1]
    want = (lax.broadcasted_iota(jnp.int32, (rows, slots), 0) + 1).astype(jnp.float32)
    receive = (want == got[which : which + 1]).astype(jnp.float32)
    values = arrived[:, which].reshape(slots, arrived.shape[-1])
    return jnp.dot(receive, values, precision=HIGHEST, preferred_element_type=jnp.float32)


def pack_into(select, field, packed):
    rows = jnp.dot(select[...], field[0], precision=HIGHEST, preferred_element_type=jnp.float32)
    tiles, _, capacity, lanes = packed.shape
    rows = rows.reshape(tiles, capacity, lanes)
    packed[:, 0] = rows
    packed[: tiles - 1, 1] = rows[1:]
    packed[tiles - 1, 1] = jnp.zeros((capacity, lanes), jnp.float32)


def pack_kernel(select, field, packed):
    pack_into(select, field, packed)


def index_kernel(tiles_count, capacity, tile, row, select, dest):
    rows = tile.shape[-1]
    slots = tiles_count * capacity
    lower = lax.broadcasted_iota(jnp.int32, (rows, rows), 0)
    upper = lax.broadcasted_iota(jnp.int32, (rows, rows), 1)
    earlier = (lower < upper).astype(jnp.float32)
    hot = lax.broadcasted_iota(jnp.int32, (tiles_count, rows), 0) == tile[...]
    hot = hot.astype(jnp.float32)
    before = jnp.dot(hot, earlier, precision=HIGHEST, preferred_element_type=jnp.float32)
    position = jnp.sum(before * hot, axis=0, keepdims=True).astype(jnp.int32)
    slot = tile[...] * capacity + position
    chosen = (lax.broadcasted_iota(jnp.int32, (slots, rows), 0) == slot).astype(jnp.float32)
    select[...] = chosen
    wanted = jnp.broadcast_to((row[...] + 1).astype(jnp.float32), (8, rows))
    found = lax.dot_general(
        wanted,
        chosen,
        (((1,), (1,)), ((), ())),
        precision=HIGHEST,
        preferred_element_type=jnp.float32,
    )
    dest[...] = found[0:1]


def start_fetch(flags, choices, buffer, sem):
    count = len(choices)
    for role, (part, index) in enumerate(choices):
        mine = flags[3] == role if role < count - 1 else flags[3] >= role

        @pl.when(mine)
        def _():
            pltpu.make_async_copy(part.at[index], buffer, sem).start()

    part, index = choices[0]
    return pltpu.make_async_copy(part.at[index], buffer, sem)


def begin_kernel(indices, *refs):
    count = len(indices)
    flags, parts = refs[0], refs[1 : 1 + count]
    out, to_chip, to_hop, sem = refs[1 + count :]
    start_fetch(flags, list(zip(parts, indices)), out, sem).wait()
    emit_halos(flags, out, to_chip, to_hop)


def chain_kernel(indices, last, *refs):
    count = len(indices)
    flags, own, chip, hop, rate, inv = refs[:6]
    parts, refs = refs[6 : 6 + count], list(refs[6 + count :])
    out, refs = refs[0], refs[1:]
    if not last:
        to_chip, to_hop, refs = refs[0], refs[1], refs[2:]
    one, two, other, keep, jump, sem = refs
    copy = start_fetch(flags, list(zip(parts, indices)), jump, sem)
    clear_edges(one, two, other)
    load_field(flags, own, chip, hop, one)

    def put(p, value):
        if p == 0:
            copy.wait()
        out[p] = value + jump[p]

    three(one, two, other, keep, lambda p, mid: rate[p] * mid, inv, put)
    if not last:
        emit_halos(flags, out, to_chip, to_hop)


def shards(states, sources, conductivity, gap_tile, gap_row):
    times, tiles = lax.axis_size("tm"), lax.axis_size("space")
    slices, comps, planes, rows, lanes = states.shape
    lay = Layout(times, tiles)
    capacity = max(2, 2 * rows // tiles)
    time_index, tile_index = lax.axis_index("tm"), lax.axis_index("space")
    core = time_index % 2
    block = 2 * (time_index // 2) + tile_index % 2
    tile = 2 * (tile_index // 2) + core
    last_slot = jnp.where(block == times - 1, slices - 1, -1)
    flags = jnp.stack(
        [
            core,
            (tile > 0).astype(jnp.int32),
            (tile < tiles - 1).astype(jnp.int32),
            block,
            last_slot,
            jnp.full((), slices, jnp.int32),
        ]
    ).astype(jnp.int32)
    relabel = lay.relabel()
    ext_planes = planes + 2 * (SWEEPS - 1)
    buf_planes = planes + 2 * SWEEPS
    plane = (rows, lanes)

    def cut(value, start, width, axis):
        return lax.dynamic_slice_in_dim(value, start, width, axis)

    def exchange(value, width, axis):
        top = planes - width
        return (
            send(cut(value, top * (1 - core), width, axis), lay.chip()),
            send(cut(value, top * core, width, axis), lay.hop()),
        )

    tables = send(jnp.stack([gap_tile[:, :, 0], gap_row]), relabel)
    all_0 = jnp.concatenate([states[:, 0], sources[:, 0], conductivity[None]], 0)
    all_0 = send(all_0, relabel)
    flat = (slices * (comps - 1), planes) + plane
    all_1 = jnp.concatenate([states[:, 1:].reshape(flat), sources[:, 1:].reshape(flat)], 0)
    all_1 = send(all_1, relabel)

    slots = tiles * capacity
    select, dest = run(
        functools.partial(index_kernel, tiles, capacity),
        slices,
        [each(1, rows), each(1, rows)],
        [each(slots, rows), each(1, slots)],
        [f32(slices, slots, rows), f32(slices, 1, slots)],
    )(tables[0][:, None], tables[1][:, None])
    groups = lay.columns()

    def trade(value):
        return lax.all_to_all(value, AXES, 0, 0, axis_index_groups=groups, tiled=True)

    dest = jnp.swapaxes(dest.reshape(slices, tiles, capacity), 0, 1)
    above = jnp.concatenate([dest[1:], jnp.zeros_like(dest[:1])], 0)
    got = trade(jnp.stack([dest, above], 2))
    got = got.transpose(1, 2, 0, 3).reshape(slices, 2, slots)

    chip_0, hop_0 = exchange(all_0, SWEEPS, 1)
    chip_1, hop_1 = exchange(all_1, SWEEPS, 1)
    count_0, count_1 = slices, slices * (comps - 1)

    def parts_of(at):
        return [each(planes, *plane, at=at)] + [each(SWEEPS, *plane, at=at)] * 2

    fine_rate, fine_inv, coarse_rate, coarse_inv = run(
        conduct_kernel,
        1,
        [SCALARS] + parts_of(2 * count_0),
        [whole(ext_planes, *plane)] * 4,
        [f32(ext_planes, *plane)] * 4,
    )(flags, all_0, chip_0, hop_0)

    def widen(fields, chip, hop, count):
        return run(
            widen_kernel,
            count,
            [SCALARS] + parts_of(count) + [whole(ext_planes, *plane)],
            each(ext_planes, *plane),
            f32(count, ext_planes, *plane),
        )(flags, fields, chip, hop, fine_inv)

    buffers = [pltpu.VMEM((buf_planes, rows + 2 * PAD, lanes), jnp.float32)] * 3 + [
        pltpu.VMEM((ext_planes, *plane), jnp.float32)
    ]
    packed_shape = (tiles, slices, 2, capacity, lanes)
    packed_spec = pl.BlockSpec((tiles, None, 2, capacity, lanes), lambda i: (0, i, 0, 0, 0))

    def fine(step, count, field, chip, hop, source, arrived=None, old=None):
        first, last = step == 0, step == STEPS - 1
        coupled = arrived is not None
        args = [flags, field, chip, hop, source, fine_rate, fine_inv]
        ins = [
            SCALARS,
            each(planes, *plane),
            each(SWEEPS, *plane),
            each(SWEEPS, *plane),
            each(ext_planes, *plane),
            whole(ext_planes, *plane),
            whole(ext_planes, *plane),
        ]
        outs, shapes = [each(planes, *plane)], [f32(count, planes, *plane)]
        if coupled:
            args += [got, arrived]
            ins += [each(2, slots), packed_spec]
            if not last:
                args.append(select)
                ins.append(each(slots, rows))
        if first:
            args += [coarse_rate, coarse_inv]
            ins += [whole(ext_planes, *plane)] * 2
        if last:
            args.append(old)
            ins.append(each(planes, *plane))
        if not last:
            outs += [each(SWEEPS, *plane)] * 2
            shapes += [f32(count, SWEEPS, *plane)] * 2
            if coupled:
                outs.append(packed_spec)
                shapes.append(f32(*packed_shape))
        if first:
            outs.append(each(planes, *plane))
            shapes.append(f32(count, planes, *plane))
        return run(
            functools.partial(fine_kernel, first, last, coupled, count // slices),
            count,
            ins,
            outs,
            shapes,
            buffers,
        )(*args)

    packed = run(
        pack_kernel,
        slices,
        [each(slots, rows), each(planes, *plane)],
        packed_spec,
        f32(*packed_shape),
    )(select, all_0)
    field_0, wide_0 = all_0, widen(all_0, chip_0, hop_0, count_0)
    field_1, wide_1 = all_1, widen(all_1, chip_1, hop_1, count_1)
    old_0 = old_1 = None
    for step in range(STEPS):
        arrived = trade(packed)
        result_0 = fine(step, count_0, field_0, chip_0, hop_0, wide_0, arrived, old_0)
        result_1 = fine(step, count_1, field_1, chip_1, hop_1, wide_1, None, old_1)
        field_0, field_1 = result_0[0], result_1[0]
        if step == 0:
            old_0, old_1 = result_0[4], result_1[3]
        if step < STEPS - 1:
            packed = result_0[3]
            chip_0, hop_0 = send(result_0[1], lay.chip()), send(result_0[2], lay.hop())
            chip_1, hop_1 = send(result_1[1], lay.chip()), send(result_1[2], lay.hop())

    others = comps - 1
    by_comp = field_1.reshape(slices, others, planes, *plane)

    def component(role):
        index = jnp.clip(role - 1, 0, others - 1)
        return lax.dynamic_index_in_dim(by_comp, index, 1, keepdims=False)

    end = times - 1
    final = {}
    for role in range(comps):
        if role == 0:
            value = field_0[slices - 1 : slices]
        else:
            at = (slices - 1) * others + role - 1
            value = field_1[at : at + 1]
        final[role] = send(value, lay.move(end, role))
    gathered = {}
    for source in range(end):
        whole_block = field_0 if source == 0 else send(field_0, lay.move(source, 0))
        for slot in range(slices):
            gathered[source, slot] = (whole_block, slot)
    for slot in range(slices - 1):
        gathered[end, slot] = (send(field_0[slot : slot + 1], lay.move(end, 0)), 0)
    spread = {
        k: send(component(block ^ k), lay.spread(k, range(1, comps))) for k in range(1, times)
    }

    def choices(source, slot):
        found = [gathered[source, slot]]
        for role in range(1, comps):
            if role == source:
                found.append((field_1, slot * others + role - 1))
            else:
                found.append((spread[role ^ source], slot))
        return [part for part, _ in found], [index for _, index in found]

    anywhere = [pl.BlockSpec(memory_space=pl.ANY)] * comps
    halo_specs = [whole(SWEEPS, *plane)] * 2
    halo_shapes = [f32(SWEEPS, *plane)] * 2
    dma = pltpu.SemaphoreType.DMA(())
    roles = range(comps)
    total = times * slices
    parts, indices = [final[role] for role in range(comps)], [0] * comps
    new, chip, hop = run(
        functools.partial(begin_kernel, indices),
        1,
        [SCALARS] + anywhere,
        [whole(planes, *plane)] + halo_specs,
        [f32(planes, *plane)] + halo_shapes,
        [dma],
    )(flags, *parts)
    news = [new]
    for j in range(total - 1):
        chip, hop = send(chip, lay.chip(roles)), send(hop, lay.hop(roles))
        last = j == total - 2
        parts, indices = choices(j // slices, j % slices)
        result = run(
            functools.partial(chain_kernel, indices, last),
            1,
            [SCALARS, whole(planes, *plane)]
            + halo_specs
            + [whole(ext_planes, *plane)] * 2
            + anywhere,
            [whole(planes, *plane)] + ([] if last else halo_specs),
            [f32(planes, *plane)] + ([] if last else halo_shapes),
            buffers + [pltpu.VMEM((planes, *plane), jnp.float32), dma],
        )(flags, new, chip, hop, coarse_rate, coarse_inv, *parts)
        new = result[0]
        if not last:
            chip, hop = result[1:]
        news.append(new)

    early = total - slices
    ready = jnp.stack(news[:early]).reshape(end, slices, planes, *plane)
    back = []
    for k in range(times):
        value = lax.dynamic_index_in_dim(ready, jnp.minimum(block ^ k, end - 1), 0, keepdims=False)
        back.append(send(value, lay.home(k, comps)))
    back = jnp.stack(back)
    result = []
    for comp in range(comps):
        pairs = lay.home_last(comp)
        late = jnp.stack([send(news[early + slot], pairs) for slot in range(slices)])
        soon = lax.dynamic_index_in_dim(back, time_index ^ comp, 0, keepdims=False)
        result.append(jnp.where(time_index == end, late, soon))
    return jnp.stack(result, axis=1)


def solution(mesh):
    placed = (
        P("tm", None, "space", None, None),
        P("tm", None, "space", None, None),
        P("space", None, None),
        P("tm", "space", None),
        P("tm", "space"),
    )

    return jax.shard_map(
        shards,
        mesh=mesh,
        in_specs=placed,
        out_specs=P("tm", None, "space", None, None),
        check_vma=False,
    )
```

```python
import functools

import jax
import jax.numpy as jnp
from jax import lax
from jax.experimental import pallas as pl
from jax.experimental.pallas import tpu as pltpu
from jax.sharding import PartitionSpec as P


STEPS = 4
SWEEPS = 3

inverse_step = 2.0
gap_gain = 1.0

AXES = ("tm", "space")
HIGHEST = lax.Precision.HIGHEST
PAD = 8


class Layout:
    def __init__(self, times, tiles):
        self.times, self.tiles = times, tiles
        self.all = [(t // 2, t % 2, s // 2, s % 2) for t in range(times) for s in range(tiles)]

    def number(self, ht, c, hs, y):
        return (2 * ht + c) * self.tiles + 2 * hs + y

    def at(self, block, tile):
        return self.number(block // 2, tile % 2, tile // 2, block % 2)

    def relabel(self):
        return [(self.number(h, c, z, y), self.number(h, y, z, c)) for h, c, z, y in self.all]

    def pairs(self, shift_of, blocks=None):
        found = []
        for block in range(self.times) if blocks is None else blocks:
            for tile in range(self.tiles):
                other = shift_of(tile)
                if 0 <= other < self.tiles:
                    found.append((self.at(block, tile), self.at(block, other)))
        return found

    def chip(self, blocks=None):
        return self.pairs(lambda tile: tile ^ 1, blocks)

    def hop(self, blocks=None):
        return self.pairs(lambda tile: tile + 1 if tile % 2 else tile - 1, blocks)

    def down(self):
        return self.pairs(lambda tile: tile - 1)

    def columns(self):
        return [[self.at(block, tile) for tile in range(self.tiles)] for block in range(self.times)]

    def spread(self, k, roles):
        return [
            (self.at(role ^ k, tile), self.at(role, tile))
            for role in roles
            for tile in range(self.tiles)
            if role ^ k < self.times
        ]

    def move(self, block, role):
        return [(self.at(block, tile), self.at(role, tile)) for tile in range(self.tiles)]

    def home(self, k, roles):
        return [
            (self.at(role, tile), (role ^ k) * self.tiles + tile)
            for role in range(roles)
            for tile in range(self.tiles)
            if role ^ k < self.times - 1
        ]

    def home_last(self, role):
        return [
            (self.at(role, tile), (self.times - 1) * self.tiles + tile)
            for tile in range(self.tiles)
        ]


def send(value, pairs):
    return lax.ppermute(value, AXES, pairs)


def f32(*shape):
    return jax.ShapeDtypeStruct(shape, jnp.float32)


def whole(*shape):
    return pl.BlockSpec(shape, lambda i: (0,) * len(shape))


def each(*shape, at=0):
    return pl.BlockSpec((None,) + shape, lambda i: (i + at,) + (0,) * len(shape))


SCALARS = pl.BlockSpec(memory_space=pltpu.SMEM)


RESIDENT = pl.BlockSpec(memory_space=pltpu.VMEM)
GRANT = 20 * 2**20


def run(kernel, grid, in_specs, out_specs, out_shape, scratch=()):
    return pl.pallas_call(
        kernel,
        grid=(grid,) if grid else (),
        compiler_params=pltpu.CompilerParams(vmem_limit_bytes=GRANT),
        in_specs=in_specs,
        out_specs=out_specs,
        out_shape=out_shape,
        scratch_shapes=list(scratch),
    )


def join(flags, own, chip, hop, wide, put):
    count, held = own.shape[0], chip.shape[0]
    put(wide, own[...])

    @pl.when(flags[0] == 0)
    def _():
        put(0, hop[held - wide :])
        put(wide + count, chip[:wide])

    @pl.when(flags[0] != 0)
    def _():
        put(0, chip[held - wide :])
        put(wide + count, hop[:wide])


def conduct_kernel(flags, own, chip, hop, fine_rate, fine_inv, coarse_rate, coarse_inv):
    def put(start, planes):
        fine_rate[start : start + planes.shape[0]] = planes

    count = own.shape[0]
    wide = (fine_rate.shape[0] - count) // 2
    join(flags, own, chip, hop, wide, put)
    for plane in range(2 * wide + count):
        inside = 1
        if plane < wide:
            inside = flags[1]
        elif plane >= wide + count:
            inside = flags[2]
        mask = jnp.full(own.shape[1:], inside, jnp.int32) != 0
        rate = inverse_step * fine_rate[plane]
        inv = jnp.where(mask, 1.0 / (rate + 6.0), 0.0)
        fine_inv[plane] = inv
        fine_rate[plane] = rate * inv
        rate = rate / STEPS
        inv = jnp.where(mask, 1.0 / (rate + 6.0), 0.0)
        coarse_inv[plane] = inv
        coarse_rate[plane] = rate * inv


def sweep(src, base, inv, low, high, emit):
    rows, lanes = inv.shape[1:]
    lane = lax.broadcasted_iota(jnp.int32, (rows, lanes), 1)
    left_edge, right_edge = lane == 0, lane == lanes - 1
    for p in range(low, high):
        mid = src[p, PAD : PAD + rows, :]
        total = src[p - 1, PAD : PAD + rows, :] + src[p + 1, PAD : PAD + rows, :]
        total = total + (src[p, PAD - 1 : PAD - 1 + rows, :] + src[p, PAD + 1 : PAD + 1 + rows, :])
        left = jnp.where(left_edge, 0.0, pltpu.roll(mid, 1, 1))
        right = jnp.where(right_edge, 0.0, pltpu.roll(mid, lanes - 1, 1))
        emit(p, base(p - 1, mid) + (total + (left + right)) * inv[p - 1])


def three(start, work, other, keep, first_base, inv, finish):
    planes, rows = start.shape[0], inv.shape[1]

    def make(p, mid):
        value = first_base(p, mid)
        if 1 <= p < inv.shape[0] - 1:
            keep[p] = value
        return value

    def to(buffer):
        def emit(p, value):
            buffer[p, PAD : PAD + rows, :] = value

        return emit

    sweep(start, make, inv, 1, planes - 1, to(work))
    sweep(work, lambda p, mid: keep[p], inv, 2, planes - 2, to(other))
    sweep(other, lambda p, mid: keep[p], inv, SWEEPS, planes - SWEEPS, lambda p, v: finish(p - SWEEPS, v))


def clear_edges(*buffers):
    for buffer in buffers:
        rows = buffer.shape[1] - 2 * PAD
        zero = jnp.zeros((buffer.shape[0], PAD, buffer.shape[2]), jnp.float32)
        buffer[:, 0:PAD, :] = zero
        buffer[:, PAD + rows :, :] = zero


def load_field(flags, own, chip, hop, buffer):
    rows = own.shape[1]

    def put(start, planes):
        buffer[start : start + planes.shape[0], PAD : PAD + rows, :] = planes

    join(flags, own, chip, hop, chip.shape[0], put)


def emit_halos(flags, out, to_chip, to_hop):
    core = flags[0]
    to_chip[...] = out[pl.ds(1 - core, SWEEPS)]
    to_hop[...] = out[pl.ds(core, SWEEPS)]


def fine_kernel(first, last, coupled, per, *refs):
    refs = list(refs)
    flags, own, chip, hop, source = refs[:5]
    refs = refs[5:]
    if first:
        source_parts, refs = [source] + refs[:2], refs[2:]
    rate, inv, refs = refs[0], refs[1], refs[2:]
    if coupled:
        got, arrived, refs = refs[0], refs[1], refs[2:]
    if coupled and not last:
        select, refs = refs[0], refs[1:]
    if first:
        coarse_rate, coarse_inv, refs = refs[0], refs[1], refs[2:]
    if last:
        old, refs = refs[0], refs[1:]
    out, refs = refs[0], refs[1:]
    if not last:
        to_chip, to_hop, refs = refs[0], refs[1], refs[2:]
    if coupled and not last:
        packed, refs = refs[0], refs[1:]
    if first:
        old_out, source, refs = refs[0], refs[1], refs[2:]
    one, two, other, keep = refs[:4]
    wide = (inv.shape[0] - own.shape[0]) // 2

    @pl.when(pl.program_id(0) == 0)
    def _():
        clear_edges(one, two, other)

    load_field(flags, own, chip, hop, one)
    if first:

        def put_source(start, planes):
            stop = start + planes.shape[0]
            source[start:stop] = planes * inv[start:stop]

        join(flags, *source_parts, wide, put_source)

        def put_old(p, value):
            old_out[p] = value

        three(one, two, other, keep, lambda p, mid: coarse_rate[p] * mid, coarse_inv, put_old)

    gaps = {}
    if coupled:
        for which in range(2):
            gap = unpacked(got, arrived, which, own.shape[1])
            gaps[wide + which * own.shape[0]] = gap_gain * gap

    def base(p, mid):
        value = rate[p] * mid + source[p]
        if p in gaps:
            value = value + gaps[p] * inv[p]
        return value

    factor = jnp.where(pl.program_id(0) // per == flags[4], 0.0, 1.0)

    def put(p, value):
        if last:
            value = value - factor * old[p]
        out[p] = value

    three(one, two, other, keep, base, inv, put)
    if not last:
        emit_halos(flags, out, to_chip, to_hop)
    if coupled and not last:
        pack_into(select, out, packed)


def unpacked(got, arrived, which, rows):
    slots = got.shape[1]
    want = (lax.broadcasted_iota(jnp.int32, (rows, slots), 0) + 1).astype(jnp.float32)
    receive = (want == got[which : which + 1]).astype(jnp.float32)
    values = arrived[:, which].reshape(slots, arrived.shape[-1])
    return jnp.dot(receive, values, precision=HIGHEST, preferred_element_type=jnp.float32)


def pack_into(select, field, packed):
    rows = jnp.dot(select[...], field[0], precision=HIGHEST, preferred_element_type=jnp.float32)
    tiles, _, capacity, lanes = packed.shape
    rows = rows.reshape(tiles, capacity, lanes)
    packed[:, 0] = rows
    packed[: tiles - 1, 1] = rows[1:]
    packed[tiles - 1, 1] = jnp.zeros((capacity, lanes), jnp.float32)


def pack_kernel(select, field, packed):
    pack_into(select, field, packed)


def index_kernel(tiles_count, capacity, tile, row, select, dest):
    rows = tile.shape[-1]
    slots = tiles_count * capacity
    lower = lax.broadcasted_iota(jnp.int32, (rows, rows), 0)
    upper = lax.broadcasted_iota(jnp.int32, (rows, rows), 1)
    earlier = (lower < upper).astype(jnp.float32)
    hot = lax.broadcasted_iota(jnp.int32, (tiles_count, rows), 0) == tile[...]
    hot = hot.astype(jnp.float32)
    before = jnp.dot(hot, earlier, precision=HIGHEST, preferred_element_type=jnp.float32)
    position = jnp.sum(before * hot, axis=0, keepdims=True).astype(jnp.int32)
    slot = tile[...] * capacity + position
    chosen = (lax.broadcasted_iota(jnp.int32, (slots, rows), 0) == slot).astype(jnp.float32)
    select[...] = chosen
    wanted = jnp.broadcast_to((row[...] + 1).astype(jnp.float32), (8, rows))
    found = lax.dot_general(
        wanted,
        chosen,
        (((1,), (1,)), ((), ())),
        precision=HIGHEST,
        preferred_element_type=jnp.float32,
    )
    dest[...] = found[0:1]


def start_fetch(flags, choices, buffer, sem):
    count = len(choices)
    for role, (part, index) in enumerate(choices):
        mine = flags[3] == role if role < count - 1 else flags[3] >= role

        @pl.when(mine)
        def _():
            pltpu.make_async_copy(part.at[index], buffer, sem).start()

    part, index = choices[0]
    return pltpu.make_async_copy(part.at[index], buffer, sem)


def begin_kernel(indices, *refs):
    count = len(indices)
    flags, parts = refs[0], refs[1 : 1 + count]
    out, to_chip, to_hop, sem = refs[1 + count :]
    start_fetch(flags, list(zip(parts, indices)), out, sem).wait()
    emit_halos(flags, out, to_chip, to_hop)


def chain_kernel(indices, last, *refs):
    count = len(indices)
    flags, own, chip, hop, rate, inv = refs[:6]
    parts, refs = refs[6 : 6 + count], list(refs[6 + count :])
    out, refs = refs[0], refs[1:]
    if not last:
        to_chip, to_hop, refs = refs[0], refs[1], refs[2:]
    one, two, other, keep, jump, sem = refs
    copy = start_fetch(flags, list(zip(parts, indices)), jump, sem)
    clear_edges(one, two, other)
    load_field(flags, own, chip, hop, one)

    def put(p, value):
        if p == 0:
            copy.wait()
        out[p] = value + jump[p]

    three(one, two, other, keep, lambda p, mid: rate[p] * mid, inv, put)
    if not last:
        emit_halos(flags, out, to_chip, to_hop)


def shards(states, sources, conductivity, gap_tile, gap_row):
    times, tiles = lax.axis_size("tm"), lax.axis_size("space")
    slices, comps, planes, rows, lanes = states.shape
    lay = Layout(times, tiles)
    capacity = max(2, 2 * rows // tiles)
    time_index, tile_index = lax.axis_index("tm"), lax.axis_index("space")
    core = time_index % 2
    block = 2 * (time_index // 2) + tile_index % 2
    tile = 2 * (tile_index // 2) + core
    last_slot = jnp.where(block == times - 1, slices - 1, -1)
    flags = jnp.stack(
        [
            core,
            (tile > 0).astype(jnp.int32),
            (tile < tiles - 1).astype(jnp.int32),
            block,
            last_slot,
            jnp.full((), slices, jnp.int32),
        ]
    ).astype(jnp.int32)
    relabel = lay.relabel()
    ext_planes = planes + 2 * (SWEEPS - 1)
    buf_planes = planes + 2 * SWEEPS
    plane = (rows, lanes)

    def cut(value, start, width, axis):
        return lax.dynamic_slice_in_dim(value, start, width, axis)

    def exchange(value, width, axis):
        top = planes - width
        return (
            send(cut(value, top * (1 - core), width, axis), lay.chip()),
            send(cut(value, top * core, width, axis), lay.hop()),
        )

    tables = send(jnp.stack([gap_tile[:, :, 0], gap_row]), relabel)
    all_0 = jnp.concatenate([states[:, 0], sources[:, 0], conductivity[None]], 0)
    all_0 = send(all_0, relabel)
    flat = (slices * (comps - 1), planes) + plane
    all_1 = jnp.concatenate([states[:, 1:].reshape(flat), sources[:, 1:].reshape(flat)], 0)
    all_1 = send(all_1, relabel)

    slots = tiles * capacity
    select, dest = run(
        functools.partial(index_kernel, tiles, capacity),
        slices,
        [each(1, rows), each(1, rows)],
        [each(slots, rows), each(1, slots)],
        [f32(slices, slots, rows), f32(slices, 1, slots)],
    )(tables[0][:, None], tables[1][:, None])
    groups = lay.columns()

    def trade(value):
        return lax.all_to_all(value, AXES, 0, 0, axis_index_groups=groups, tiled=True)

    dest = jnp.swapaxes(dest.reshape(slices, tiles, capacity), 0, 1)
    above = jnp.concatenate([dest[1:], jnp.zeros_like(dest[:1])], 0)
    got = trade(jnp.stack([dest, above], 2))
    got = got.transpose(1, 2, 0, 3).reshape(slices, 2, slots)

    chip_0, hop_0 = exchange(all_0, SWEEPS, 1)
    chip_1, hop_1 = exchange(all_1, SWEEPS, 1)
    count_0, count_1 = slices, slices * (comps - 1)

    def parts_of(at):
        return [each(planes, *plane, at=at)] + [each(SWEEPS, *plane, at=at)] * 2

    fine_rate, fine_inv, coarse_rate, coarse_inv = run(
        conduct_kernel,
        1,
        [SCALARS] + parts_of(2 * count_0),
        [whole(ext_planes, *plane)] * 4,
        [f32(ext_planes, *plane)] * 4,
    )(flags, all_0, chip_0, hop_0)

    buffers = [pltpu.VMEM((buf_planes, rows + 2 * PAD, lanes), jnp.float32)] * 3 + [
        pltpu.VMEM((ext_planes, *plane), jnp.float32)
    ]
    packed_shape = (tiles, slices, 2, capacity, lanes)
    packed_spec = pl.BlockSpec((tiles, None, 2, capacity, lanes), lambda i: (0, i, 0, 0, 0))

    def fine(step, count, field, chip, hop, source, arrived=None, old=None):
        first, last = step == 0, step == STEPS - 1
        coupled = arrived is not None
        args, ins = [flags, field, chip, hop], [SCALARS] + parts_of(0)
        if first:
            args += [field, chip, hop]
            ins += parts_of(count)
        else:
            args.append(source)
            ins.append(each(ext_planes, *plane))
        args += [fine_rate, fine_inv]
        ins += [whole(ext_planes, *plane)] * 2
        outs, shapes = [each(planes, *plane)], [f32(count, planes, *plane)]
        if coupled:
            args += [got, arrived]
            ins += [each(2, slots), packed_spec]
            if not last:
                args.append(select)
                ins.append(each(slots, rows))
        if first:
            args += [coarse_rate, coarse_inv]
            ins += [whole(ext_planes, *plane)] * 2
        if last:
            args.append(old)
            ins.append(each(planes, *plane))
        if not last:
            outs += [each(SWEEPS, *plane)] * 2
            shapes += [f32(count, SWEEPS, *plane)] * 2
            if coupled:
                outs.append(packed_spec)
                shapes.append(f32(*packed_shape))
        if first:
            outs += [each(planes, *plane), each(ext_planes, *plane)]
            shapes += [f32(count, planes, *plane), f32(count, ext_planes, *plane)]
        return run(
            functools.partial(fine_kernel, first, last, coupled, count // slices),
            count,
            ins,
            outs,
            shapes,
            buffers,
        )(*args)

    packed = run(
        pack_kernel,
        slices,
        [each(slots, rows), each(planes, *plane)],
        packed_spec,
        f32(*packed_shape),
    )(select, all_0)
    field_0, field_1, wide_0, wide_1 = all_0, all_1, None, None
    old_0 = old_1 = None
    for step in range(STEPS):
        arrived = trade(packed)
        result_0 = fine(step, count_0, field_0, chip_0, hop_0, wide_0, arrived, old_0)
        result_1 = fine(step, count_1, field_1, chip_1, hop_1, wide_1, None, old_1)
        field_0, field_1 = result_0[0], result_1[0]
        if step == 0:
            old_0, wide_0 = result_0[4:]
            old_1, wide_1 = result_1[3:]
        if step < STEPS - 1:
            packed = result_0[3]
            chip_0, hop_0 = send(result_0[1], lay.chip()), send(result_0[2], lay.hop())
            chip_1, hop_1 = send(result_1[1], lay.chip()), send(result_1[2], lay.hop())

    others = comps - 1
    by_comp = field_1.reshape(slices, others, planes, *plane)

    def component(role):
        index = jnp.clip(role - 1, 0, others - 1)
        return lax.dynamic_index_in_dim(by_comp, index, 1, keepdims=False)

    end = times - 1
    final = {}
    for role in range(comps):
        if role == 0:
            value = field_0[slices - 1 : slices]
        else:
            at = (slices - 1) * others + role - 1
            value = field_1[at : at + 1]
        final[role] = send(value, lay.move(end, role))
    gathered = {}
    for source in range(end):
        whole_block = field_0 if source == 0 else send(field_0, lay.move(source, 0))
        for slot in range(slices):
            gathered[source, slot] = (whole_block, slot)
    for slot in range(slices - 1):
        gathered[end, slot] = (send(field_0[slot : slot + 1], lay.move(end, 0)), 0)
    spread = {
        k: send(component(block ^ k), lay.spread(k, range(1, comps))) for k in range(1, times)
    }

    def choices(source, slot):
        found = [gathered[source, slot]]
        for role in range(1, comps):
            if role == source:
                found.append((field_1, slot * others + role - 1))
            else:
                found.append((spread[role ^ source], slot))
        return [part for part, _ in found], [index for _, index in found]

    anywhere = [pl.BlockSpec(memory_space=pl.ANY)] * comps
    halo_specs = [RESIDENT] * 2
    halo_shapes = [f32(SWEEPS, *plane)] * 2
    dma = pltpu.SemaphoreType.DMA(())
    roles = range(comps)
    total = times * slices
    parts, indices = [final[role] for role in range(comps)], [0] * comps
    new, chip, hop = run(
        functools.partial(begin_kernel, indices),
        0,
        [SCALARS] + anywhere,
        [RESIDENT] + halo_specs,
        [f32(planes, *plane)] + halo_shapes,
        [dma],
    )(flags, *parts)
    news = [new]
    for j in range(total - 1):
        chip, hop = send(chip, lay.chip(roles)), send(hop, lay.hop(roles))
        last = j == total - 2
        parts, indices = choices(j // slices, j % slices)
        result = run(
            functools.partial(chain_kernel, indices, last),
            0,
            [SCALARS] + [RESIDENT] * 5 + anywhere,
            [RESIDENT] + ([] if last else halo_specs),
            [f32(planes, *plane)] + ([] if last else halo_shapes),
            buffers + [pltpu.VMEM((planes, *plane), jnp.float32), dma],
        )(flags, new, chip, hop, coarse_rate, coarse_inv, *parts)
        new = result[0]
        if not last:
            chip, hop = result[1:]
        news.append(new)

    early = total - slices
    ready = jnp.stack(news[:early]).reshape(end, slices, planes, *plane)
    back = []
    for k in range(times):
        value = lax.dynamic_index_in_dim(ready, jnp.minimum(block ^ k, end - 1), 0, keepdims=False)
        back.append(send(value, lay.home(k, comps)))
    back = jnp.stack(back)
    result = []
    for comp in range(comps):
        pairs = lay.home_last(comp)
        late = []
        for slot in range(slices):
            late.append(send(news[early + slot], pairs))
        late = jnp.stack(late)
        soon = lax.dynamic_index_in_dim(back, time_index ^ comp, 0, keepdims=False)
        result.append(jnp.where(time_index == end, late, soon))
    return jnp.stack(result, axis=1)


def solution(mesh):
    placed = (
        P("tm", None, "space", None, None),
        P("tm", None, "space", None, None),
        P("space", None, None),
        P("tm", "space", None),
        P("tm", "space"),
    )

    return jax.shard_map(
        shards,
        mesh=mesh,
        in_specs=placed,
        out_specs=P("tm", None, "space", None, None),
        check_vma=False,
    )
```
